32 devices in a mesh: group: 2 (over x), expert: 16 (over z, y, core).
Axes of the slice: x: 2, y: 2, z: 4, core: 2. Of those that a mesh axis runs over, the one named last changes fastest.
Arguments:
- tokens: bfloat16 [4096, 3584], P(('group', 'expert')), parts along dimension 0, may hold values from -6 to 6
- routes: int32 [4096, 1], P(('group', 'expert')), parts along dimension 0, may hold values from 0 to 3; in each aligned block of 128 rows (0 to 127, 128 to 255, ...) at most 64 rows name the same one
- gate_weights: float32 [4096, 1], P(('group', 'expert')), parts along dimension 0, may hold values from 0.25 to 1
- w_gate: bfloat16 [16, 3584, 512], P('expert'), may hold values from -0.09375 to 0.09375
- w_up: bfloat16 [16, 3584, 512], P('expert'), may hold values from -0.09375 to 0.09375
- w_down: bfloat16 [16, 512, 3584], P('expert'), may hold values from -0.125 to 0.125
Outputs:
- layer_out: bfloat16 [4096, 3584], P(('group', 'expert')), parts along dimension 0
The draws below stay inside these ranges and needn't reach their ends.
There are 2 independent parts, one for each index of `group`. The reference program is written for one: setup_inputs(seed, part) draws one part's arguments, and reference() takes and returns one part's arrays. A program takes and returns all parts, laid end to end along the dimension named above; an argument that names none is the same for every part. Nothing has to cross between parts.
Inputs may be any that keep to these rules, and one draw needn't show every extreme that they name: `routes`: each token names one of the 4 experts; among the 128 tokens of one device no expert is named more than 64 times, and in every draw some device names some expert exactly 64 times.
All inputs are finite; a program needn't handle non-finite values.
Results may differ from the reference program's by a relative error of at most 0.0085.
Values may be sent and summed in bfloat16 or wider, within the bound.
No kernel may reach another device: no remote copies, remote signals or barrier semaphores. Data moves between devices by JAX's collectives and lax.ppermute only.
A program may use at most 128 MiB of HBM per device.

```python
import math
import jax
import jax.numpy as jnp
import numpy as np
from jax import lax

D = 3584
FF = 2048
SPAN = 4
TOK_DEV = 128
HID_DEV = 512
EXPERTS = 4
CAP = 64
TOKENS = 2048
N_EXPERT = 16


def block_levels(key, shape, pieces, smallest, largest):
    def one(dim, blocks):
        draws = jax.random.uniform(jax.random.fold_in(jax.random.fold_in(key, 6), dim), (blocks,), jnp.float32, smallest / len(pieces), largest / len(pieces))
        return jnp.repeat(jnp.exp(draws), shape[dim] // blocks).reshape((-1,) + (1,) * (len(shape) - dim - 1))

    factor_of = one(*pieces[0])
    for cut in pieces[1:]:
        factor_of = factor_of * one(*cut)
    return factor_of


def shared_out(own_key, own, number, rows, count, top, bound, lean):
    ranking = jax.random.permutation(own_key, count)
    crowded, common = portions_of(count, rows * top, bound, lean, True), portions_of(count, rows * top, bound, lean, False)
    places = jnp.arange(count)

    def named(sizes, offset_by):
        used = int((sizes > 0).sum())
        fixed = max(1, used // 4)
        moved = fixed + (places - fixed + offset_by * (used - fixed)) % max(1, count - fixed)
        return jnp.zeros((count,), jnp.int32).at[ranking[jnp.where(places < fixed, places, moved)]].set(jnp.asarray(sizes, jnp.int32))

    sizes = jnp.where(number % 4 == 0, named(crowded, number // 4), named(common, number - number // 4 - 1))
    mixed = jax.random.permutation(jax.random.fold_in(own, 3), count)
    donor, receiver = mixed[0:count // 2 * 2:2], mixed[1:count // 2 * 2:2]
    slack = jnp.minimum(sizes[donor] - 1, bound - sizes[receiver]) // 2
    slack = jnp.where((donor == ranking[0]) | (receiver == ranking[0]) | (sizes[receiver] == 0), 0, jnp.maximum(slack, 0))
    moved = jax.random.randint(jax.random.fold_in(own, 4), (count // 2,), 0, 1 << 20) % (slack + 1)
    sizes = sizes.at[donor].add(-moved).at[receiver].add(moved)
    members = jnp.searchsorted(jnp.cumsum(sizes), jnp.arange(rows * top), side="right").astype(jnp.int32)
    grid = members.reshape(top, rows).T
    grid = grid[jax.random.permutation(jax.random.fold_in(own, 1), rows)]
    offset_by = jax.random.randint(jax.random.fold_in(own, 2), (rows, 1), 0, top)
    return jnp.take_along_axis(grid, (jnp.arange(top)[None, :] + offset_by) % top, axis=1)


def portions_of(amount, total, bound, lean, full):
    loads = [(1 << 20) // math.isqrt(rank ** lean) + 1 for rank in range(1, amount + 1)]
    largest = bound if full else min(bound, max(-(-total // amount), total * loads[0] // sum(loads)))
    least = 1 if total - largest >= amount - 1 else 0
    holding, surplus = [largest] + [least] * (amount - 1), total - largest - least * (amount - 1)
    while surplus > 0:
        free = [i for i in range(1, amount) if holding[i] < largest] or [i for i in range(1, amount) if holding[i] < bound]
        pool, remaining = sum([loads[i] for i in free]), surplus
        for i in free:
            addition = min(bound - holding[i], max(1, remaining * loads[i] // pool), surplus)
            holding[i] = holding[i] + addition
            surplus = surplus - addition
    return np.array(holding)


def bell_draw(stream_key, extent, width, limit, shards=(), held_as=jnp.bfloat16):
    loudness = block_levels(stream_key, extent, shards, -0.22, 0.18) if shards else 1.0
    array = jax.random.normal(stream_key, extent, jnp.float32) * width * loudness
    return jnp.minimum(jnp.maximum(array, -limit), limit).astype(held_as)


def setup_inputs(seed: int = 0, part: int = 0) -> dict:
    key_of = jax.random.split(jax.random.key(seed), 7)
    part_splits = jax.random.split(jax.random.fold_in(key_of[6], part), 7)
    tokens = bell_draw(part_splits[0], (TOKENS, D), 1.0, 6.0, ((0, 16),))
    routes_keys = jax.random.split(jax.random.fold_in(part_splits[1], 1), TOKENS // TOK_DEV)
    routes_turns = jax.random.permutation(jax.random.fold_in(part_splits[1], 3), TOKENS // TOK_DEV)
    routes = jax.vmap(lambda own, number: shared_out(jax.random.fold_in(part_splits[1], 2), own, number, TOK_DEV, EXPERTS, 1, CAP, 2))(routes_keys, routes_turns).reshape((TOKENS, 1))
    gate_weights = jnp.clip(0.25 + 0.75 * jax.random.uniform(part_splits[2], (TOKENS, 1), jnp.float32) ** block_levels(part_splits[2], (TOKENS, 1), ((0, 16),), -0.2, 0.2), 0.25, 1.0)
    w_gate = bell_draw(key_of[3], (EXPERTS * SPAN, D, HID_DEV), D ** -0.5, 0.09375, ((0, 16),))
    w_up = bell_draw(key_of[4], (EXPERTS * SPAN, D, HID_DEV), D ** -0.5, 0.09375, ((0, 16),))
    w_down = bell_draw(key_of[5], (EXPERTS * SPAN, HID_DEV, D), FF ** -0.5, 0.125, ((0, 16),))
    return {"tokens": tokens, "routes": routes, "gate_weights": gate_weights, "w_gate": w_gate, "w_up": w_up, "w_down": w_down}


def expert_rows(picked, gate_part, up_part, down_part):
    summed = jnp.zeros((picked.shape[0], down_part.shape[2]), jnp.float32)
    for span_piece in range(SPAN):
        gate_val = jnp.dot(picked, gate_part[span_piece], preferred_element_type=jnp.float32)
        up_val = jnp.dot(picked, up_part[span_piece], preferred_element_type=jnp.float32)
        hidden = (jax.nn.silu(gate_val) * up_val).astype(jnp.bfloat16)
        partial_value = jnp.dot(hidden, down_part[span_piece], preferred_element_type=jnp.float32).astype(jnp.bfloat16)
        partial_value = lax.optimization_barrier(partial_value)
        summed = summed + partial_value.astype(jnp.float32)
    return summed


def reference(tokens, routes, gate_weights, w_gate, w_up, w_down):
    route_ids = routes[:, 0]
    row_limit = N_EXPERT * CAP

    def per_expert(accum_out, expert):
        chosen = jnp.nonzero(route_ids == expert, size=row_limit, fill_value=TOKENS)[0].astype(jnp.int32)
        picked = jnp.take(tokens, jnp.minimum(chosen, TOKENS - 1), axis=0)
        first_row = (expert * SPAN).astype(jnp.int32)
        gate_part = lax.dynamic_slice_in_dim(w_gate, first_row, SPAN, 0)
        up_part = lax.dynamic_slice_in_dim(w_up, first_row, SPAN, 0)
        down_part = lax.dynamic_slice_in_dim(w_down, first_row, SPAN, 0)
        result = expert_rows(picked, gate_part, up_part, down_part)
        accum_out = accum_out.at[chosen].set(result, mode="drop")
        return accum_out, None

    experts_out, unused = lax.scan(per_expert, jnp.zeros((TOKENS, D), jnp.float32), jnp.arange(EXPERTS, dtype=jnp.int32))
    return (gate_weights[:, 0:1] * experts_out).astype(jnp.bfloat16)
```

```python
import jax
import jax.numpy as jnp
from jax import lax
from jax.sharding import Mesh
from jax.sharding import PartitionSpec as P

SPAN = 4
SWAP = [(0, 1), (1, 0)]


def expert_part(rows, weights):
    total = None
    for w_gate, w_up, w_down in weights:
        gate_val = jnp.dot(rows, w_gate, preferred_element_type=jnp.float32)
        up_val = jnp.dot(rows, w_up, preferred_element_type=jnp.float32)
        hidden = (jax.nn.silu(gate_val) * up_val).astype(jnp.bfloat16)
        part = jnp.dot(hidden, w_down, preferred_element_type=jnp.float32)
        total = part if total is None else total + part
    return total


def per_device(tokens, routes, gate_weights, w_gate, w_up, w_down):
    rows = tokens.shape[0]
    experts = lax.axis_size("plane")
    capacity = 2 * rows // experts
    plane = lax.axis_index("plane")
    paired = experts & (experts - 1) == 0

    def there(k):
        return [(i, i ^ k if paired else (i + k) % experts) for i in range(experts)]

    def back(k):
        return [(b, a) for a, b in there(k)]

    partner = [lax.ppermute(w[0], "core", SWAP) for w in (w_gate, w_up, w_down)]
    weights = [(w_gate[0], w_up[0], w_down[0]), tuple(partner)]

    route = routes[:, 0]
    step = route ^ plane if paired else (route - plane) % experts
    earlier = jnp.arange(rows)[:, None] > jnp.arange(rows)[None, :]
    position = jnp.sum((earlier & (route[:, None] == route[None, :])).astype(jnp.int32), axis=1)
    slot = step * capacity + position
    wanted = (jnp.arange(experts * capacity, dtype=jnp.int32)[:, None] == slot[None, :]).astype(
        jnp.bfloat16
    )
    picks = [wanted[k * capacity : (k + 1) * capacity] for k in range(experts)]
    packed = [
        jnp.dot(pick, tokens, preferred_element_type=jnp.float32).astype(jnp.bfloat16)
        for pick in picks
    ]

    def turn(x):
        return lax.ppermute(x, "row", SWAP)

    own_turned = turn(packed[0])
    near_turned = turn(packed[1])
    far = {k: lax.ppermute(packed[k], "plane", there(k)) for k in range(2, experts)}
    near_a = lax.ppermute(packed[1], "plane", there(1))
    near_b = lax.ppermute(near_turned, "plane", there(1))

    def run(a, b):
        out = expert_part(jnp.concatenate([a, b], axis=0), weights)
        return out[:capacity], out[capacity:].astype(jnp.bfloat16)

    returned = []
    own_a, own_b = run(packed[0], own_turned)
    returned.append((0, own_a.astype(jnp.bfloat16)))
    returned.append((0, turn(own_b)))
    for k in range(2, experts):
        a, b = run(far[k], turn(far[k]))
        both = (a + turn(b).astype(jnp.float32)).astype(jnp.bfloat16)
        returned.append((k, lax.ppermute(both, "plane", back(k))))
    a, b = run(near_a, near_b)
    returned.append((1, lax.ppermute(a.astype(jnp.bfloat16), "plane", back(1))))
    returned.append((1, turn(lax.ppermute(b, "plane", back(1)))))
    total = jnp.zeros(tokens.shape, jnp.float32)
    for k, value in returned:
        total = total + lax.dot_general(
            picks[k], value, (((0,), (0,)), ((), ())), preferred_element_type=jnp.float32
        )
    return (gate_weights * total).astype(jnp.bfloat16)


def solution(mesh):
    groups, devices = mesh.shape["group"], mesh.shape["expert"]
    fine = Mesh(
        mesh.devices.reshape(groups, devices // SPAN, SPAN // 2, 2),
        ("group", "plane", "row", "core"),
    )
    every = ("group", "plane", "row", "core")
    expert = ("plane", "row", "core")
    placed = (P(every, None),) * 3 + (P(expert, None, None),) * 3
    return jax.shard_map(
        per_device, mesh=fine, in_specs=placed, out_specs=P(every, None), check_vma=False
    )
```

```python
import functools

import jax
import jax.numpy as jnp
from jax import lax
from jax.experimental import pallas as pl
from jax.experimental.pallas import tpu as pltpu
from jax.sharding import Mesh
from jax.sharding import PartitionSpec as P


SPAN = 4
SWAP = [(0, 1), (1, 0)]
VMEM = pl.BlockSpec(memory_space=pltpu.VMEM)
SMEM = pl.BlockSpec(memory_space=pltpu.SMEM)
ANY = pl.BlockSpec(memory_space=pl.ANY)


def tile_of(size, most):
    return max(t for t in range(128, most + 1, 128) if size % t == 0)


def steps_to(route, plane, experts):
    if experts & (experts - 1) == 0:
        return route ^ plane
    return lax.rem(route - plane + experts, experts)


def grids(rows):
    return [lax.broadcasted_iota(jnp.int32, (rows, rows), d) for d in range(2)]


def turned(row):
    rows = row.shape[1]
    sub, lane = grids(rows)
    wide = jnp.broadcast_to(row, (rows, rows))
    return jnp.sum(jnp.where(sub == lane, wide, jnp.zeros_like(wide)), axis=1, keepdims=True)


def slots_by_row(row, plane, experts, capacity):
    sub, lane = grids(row.shape[1])
    before = ((turned(row) == row) & (sub < lane)).astype(jnp.int32)
    position = jnp.sum(before, axis=0, keepdims=True)
    return steps_to(row, plane, experts) * capacity + position


def pack_kernel(experts, capacity, plane_ref, routes_ref, tokens_ref, *outs):
    slot = slots_by_row(routes_ref[...], plane_ref[0], experts, capacity)
    rows, width = tokens_ref.shape
    every = lax.broadcasted_iota(jnp.int32, (experts * capacity, rows), 0)
    pick = (slot == every).astype(jnp.bfloat16)
    half = width // 2
    tile = tile_of(half, 512)
    for c in range(0, width, tile):
        part = pl.ds(c % half, tile)
        value = jnp.dot(pick, tokens_ref[:, pl.ds(c, tile)], preferred_element_type=jnp.float32)
        value = value.astype(jnp.bfloat16)
        for k in range(experts):
            outs[2 * k + c // half][:, part] = value[k * capacity : (k + 1) * capacity]


def pack(plane, routes, tokens, experts, capacity):
    rows, width = tokens.shape
    outs = pl.pallas_call(
        functools.partial(pack_kernel, experts, capacity),
        out_shape=[jax.ShapeDtypeStruct((capacity, width // 2), jnp.bfloat16)] * (2 * experts),
        in_specs=[SMEM, VMEM, VMEM],
        out_specs=[VMEM] * (2 * experts),
        cost_estimate=pl.CostEstimate(
            flops=2 * rows * experts * capacity * width,
            bytes_accessed=2 * (rows + experts * capacity) * width,
            transcendentals=0,
        ),
        compiler_params=pltpu.CompilerParams(vmem_limit_bytes=12 << 20),
        name="pack",
    )(plane, routes, tokens)
    return [tuple(outs[2 * k : 2 * k + 2]) for k in range(experts)]


def place_kernel(experts, capacity, steps, has_base, last, plane_ref, routes_ref, *refs):
    refs = list(refs)
    out = refs.pop()
    scale = turned(refs.pop(0)[...]) if last else None
    base = refs.pop(0) if has_base else None
    row = routes_ref[...]
    rows, width = out.shape
    slot = turned(slots_by_row(row, plane_ref[0], experts, capacity))
    first = lax.broadcasted_iota(jnp.int32, (rows, capacity), 1)
    pick = jnp.concatenate([(slot == first + k * capacity).astype(jnp.float32) for k in steps], axis=1)
    pick = pick.astype(jnp.bfloat16)
    half = width // 2
    tile = tile_of(half, 512)
    for c in range(0, width, tile):
        part, whole = pl.ds(c % half, tile), pl.ds(c, tile)
        data = [refs[2 * n + c // half][:, part] for n in range(len(steps))]
        value = jnp.dot(
            pick, jnp.concatenate(data, axis=0), preferred_element_type=jnp.float32
        )
        if has_base:
            value = value + base[:, whole]
        if last:
            value = scale * value
        out[:, whole] = value.astype(out.dtype)


def place(plane, routes, items, experts, base=None, scale=None):
    rows = routes.shape[1]
    capacity, half = items[0][1][0].shape
    width = 2 * half
    last = scale is not None
    operands = [plane, routes]
    if last:
        operands.append(scale)
    if base is not None:
        operands.append(base)
    for _, halves in items:
        operands += halves
    steps = [k for k, _ in items]
    return pl.pallas_call(
        functools.partial(place_kernel, experts, capacity, steps, base is not None, last),
        out_shape=jax.ShapeDtypeStruct((rows, width), jnp.bfloat16 if last else jnp.float32),
        in_specs=[SMEM] + [VMEM] * (len(operands) - 1),
        out_specs=VMEM,
        cost_estimate=pl.CostEstimate(
            flops=2 * rows * len(items) * capacity * width,
            bytes_accessed=2 * (rows + len(items) * capacity) * width,
            transcendentals=0,
        ),
        compiler_params=pltpu.CompilerParams(vmem_limit_bytes=12 << 20),
        name="place",
    )(*operands)


def stage_kernel(*refs):
    count = (len(refs) - 1) // 2
    sems = refs[-1]
    copies = [
        pltpu.make_async_copy(refs[i], refs[count + i], sems.at[i]) for i in range(count)
    ]
    for copy in copies:
        copy.start()
    for copy in copies:
        copy.wait()


def stage(arrays):
    return pl.pallas_call(
        stage_kernel,
        out_shape=[pltpu.VMEM(a.shape, a.dtype) for a in arrays],
        in_specs=[ANY] * len(arrays),
        out_specs=[VMEM] * len(arrays),
        scratch_shapes=[pltpu.SemaphoreType.DMA((len(arrays),))],
        cost_estimate=pl.CostEstimate(
            flops=0, bytes_accessed=4 * sum(a.size for a in arrays), transcendentals=0
        ),
        compiler_params=pltpu.CompilerParams(vmem_limit_bytes=4 << 20),
        name="stage",
    )(*arrays)


def expert_kernel(blocks, hid_tile, *refs):
    ins, refs = refs[: 2 * blocks], refs[2 * blocks :]
    weights, refs = refs[:6], refs[6:]
    outs, refs = refs[: 2 * blocks], refs[2 * blocks :]
    rows, hidden = refs
    capacity, half = ins[0].shape
    hid = hidden.shape[1] // 2
    for i in range(blocks):
        for c in range(2):
            rows[pl.ds(i * capacity, capacity), pl.ds(c * half, half)] = ins[2 * i + c][...]
    x = rows[...]
    for s in range(2):
        gate, up = weights[3 * s], weights[3 * s + 1]
        for h in range(0, hid, hid_tile):
            part = pl.ds(h, hid_tile)
            gate_val = jnp.dot(x, gate[:, part], preferred_element_type=jnp.float32)
            up_val = jnp.dot(x, up[:, part], preferred_element_type=jnp.float32)
            value = gate_val / (1.0 + jnp.exp(-gate_val)) * up_val
            hidden[:, pl.ds(s * hid + h, hid_tile)] = value.astype(jnp.bfloat16)
    tile = tile_of(half, 512)
    for c in range(0, 2 * half, tile):
        part, whole = pl.ds(c % half, tile), pl.ds(c, tile)
        value = jnp.dot(hidden[:, :hid], weights[2][:, whole], preferred_element_type=jnp.float32)
        value += jnp.dot(hidden[:, hid:], weights[5][:, whole], preferred_element_type=jnp.float32)
        value = value.astype(jnp.bfloat16)
        for i in range(blocks):
            outs[2 * i + c // half][:, part] = value[i * capacity : (i + 1) * capacity]


def run_expert(blocks, weights):
    capacity, half = blocks[0][0].shape
    count, total, width = len(blocks), len(blocks) * capacity, 2 * half
    hid = weights[0].shape[1]
    outs = pl.pallas_call(
        functools.partial(expert_kernel, count, tile_of(hid, 256)),
        out_shape=[jax.ShapeDtypeStruct((capacity, half), jnp.bfloat16)] * (2 * count),
        in_specs=[VMEM] * (2 * count + 6),
        out_specs=[VMEM] * (2 * count),
        scratch_shapes=[
            pltpu.VMEM((total, width), jnp.bfloat16),
            pltpu.VMEM((total, 2 * hid), jnp.bfloat16),
        ],
        compiler_params=pltpu.CompilerParams(vmem_limit_bytes=16 << 20),
        cost_estimate=pl.CostEstimate(
            flops=2 * total * width * hid * 6,
            bytes_accessed=12 * width * hid + 4 * total * width,
            transcendentals=total * hid * 2,
        ),
        name="expert",
    )(*[h for block in blocks for h in block], *weights)
    return [tuple(outs[2 * i : 2 * i + 2]) for i in range(count)]


def per_device(tokens, routes, gate_weights, w_gate, w_up, w_down):
    rows = tokens.shape[0]
    experts = lax.axis_size("plane")
    capacity = 2 * rows // experts
    paired = experts & (experts - 1) == 0
    plane = jnp.reshape(lax.axis_index("plane"), (1,)).astype(jnp.int32)
    routes, scale = routes.reshape(1, rows), gate_weights.reshape(1, rows)

    def there(k):
        return [(i, i ^ k if paired else (i + k) % experts) for i in range(experts)]

    def back(k):
        return [(b, a) for a, b in there(k)]

    def both(halves, axis, pairs):
        return tuple(lax.ppermute(x, axis, pairs) for x in halves)

    packed = pack(plane, routes, tokens, experts, capacity)
    own = both(packed[0], "row", SWAP)
    near = both(packed[1], "row", SWAP)
    far = {k: both(packed[k], "plane", there(k)) for k in range(2, experts)}
    near_a = both(packed[1], "plane", there(1))
    near_b = both(near, "plane", there(1))
    weights = [w_gate[0], w_up[0], w_down[0]]
    other = [lax.ppermute(w, "core", SWAP) for w in weights]
    weights = stage(weights)
    weights += stage(other)

    far_back = []
    for k in range(2, experts):
        turn = both(far[k], "row", SWAP)
        a, b = run_expert([far[k], turn], weights)
        b = both(b, "row", SWAP)
        total = [
            (u.astype(jnp.float32) + v.astype(jnp.float32)).astype(jnp.bfloat16)
            for u, v in zip(a, b)
        ]
        far_back.append((k, both(total, "plane", back(k))))
    own_a, own_b, a, b = run_expert([packed[0], own, near_a, near_b], weights)
    own_b = both(own_b, "row", SWAP)
    near_back_a = both(a, "plane", back(1))
    near_back_b = both(both(b, "plane", back(1)), "row", SWAP)
    early = [(0, own_a), (1, near_back_a)] + far_back[:-1]
    late = [(0, own_b), (1, near_back_b), far_back[-1]]
    base = place(plane, routes, early, experts)
    return place(plane, routes, late, experts, base, scale)


def solution(mesh):
    groups, devices = mesh.shape["group"], mesh.shape["expert"]
    experts = devices // SPAN
    fine = Mesh(
        mesh.devices.reshape(groups, experts, SPAN // 2, 2), ("group", "plane", "row", "core")
    )
    every = ("group", "plane", "row", "core")
    expert = ("plane", "row", "core")
    placed = (P(every, None),) * 3 + (P(expert, None, None),) * 3

    return jax.shard_map(
        per_device, mesh=fine, in_specs=placed, out_specs=P(every, None), check_vma=False
    )
```

```python
import functools

import jax
import jax.numpy as jnp
from jax import lax
from jax.experimental import pallas as pl
from jax.experimental.pallas import tpu as pltpu
from jax.sharding import Mesh
from jax.sharding import PartitionSpec as P


SPAN = 4
SWAP = [(0, 1), (1, 0)]
VMEM = pl.BlockSpec(memory_space=pltpu.VMEM)
SMEM = pl.BlockSpec(memory_space=pltpu.SMEM)
HBM = pl.BlockSpec(memory_space=pltpu.HBM)


def held(x):
    return pltpu.with_memory_space_constraint(x, pltpu.HBM)


def tile_of(size, most):
    return max(t for t in range(128, most + 1, 128) if size % t == 0)


def steps_to(route, plane, experts):
    if experts & (experts - 1) == 0:
        return route ^ plane
    return lax.rem(route - plane + experts, experts)


def grids(rows):
    return [lax.broadcasted_iota(jnp.int32, (rows, rows), d) for d in range(2)]


def turned(row):
    rows = row.shape[1]
    sub, lane = grids(rows)
    wide = jnp.broadcast_to(row, (rows, rows))
    return jnp.sum(jnp.where(sub == lane, wide, jnp.zeros_like(wide)), axis=1, keepdims=True)


def slots_by_row(row, plane, experts, capacity):
    sub, lane = grids(row.shape[1])
    before = ((turned(row) == row) & (sub < lane)).astype(jnp.int32)
    position = jnp.sum(before, axis=0, keepdims=True)
    return steps_to(row, plane, experts) * capacity + position


def pack_kernel(experts, capacity, plane_ref, routes_ref, tokens_ref, *refs):
    outs, (routes, tokens, sems) = refs[:-3], refs[-3:]
    rows, width = tokens.shape
    half = width // 2
    first = pltpu.make_async_copy(routes_ref, routes, sems.at[2])
    first.start()
    copies = []
    for c in range(2):
        part = pl.ds(c * half, half)
        copies.append(
            pltpu.make_async_copy(tokens_ref.at[:, part], tokens.at[:, part], sems.at[c])
        )
        copies[c].start()
    first.wait()
    slot = slots_by_row(routes[...], plane_ref[0], experts, capacity)
    every = lax.broadcasted_iota(jnp.int32, (experts * capacity, rows), 0)
    pick = (slot == every).astype(jnp.bfloat16)
    tile = tile_of(half, 512)
    for c in range(0, width, tile):
        if c % half == 0:
            copies[c // half].wait()
        part = pl.ds(c % half, tile)
        value = jnp.dot(pick, tokens[:, pl.ds(c, tile)], preferred_element_type=jnp.float32)
        value = value.astype(jnp.bfloat16)
        for k in range(experts):
            outs[2 * k + c // half][:, part] = value[k * capacity : (k + 1) * capacity]


def pack(plane, routes, tokens, experts, capacity):
    rows, width = tokens.shape
    outs = pl.pallas_call(
        functools.partial(pack_kernel, experts, capacity),
        out_shape=[jax.ShapeDtypeStruct((capacity, width // 2), jnp.bfloat16)] * (2 * experts),
        in_specs=[SMEM, HBM, HBM],
        out_specs=[VMEM] * (2 * experts),
        scratch_shapes=[
            pltpu.VMEM(routes.shape, routes.dtype),
            pltpu.VMEM(tokens.shape, tokens.dtype),
            pltpu.SemaphoreType.DMA((3,)),
        ],
        cost_estimate=pl.CostEstimate(
            flops=2 * rows * experts * capacity * width,
            bytes_accessed=2 * (rows + experts * capacity) * width,
            transcendentals=0,
        ),
        compiler_params=pltpu.CompilerParams(vmem_limit_bytes=12 << 20),
        name="pack",
    )(plane, held(routes), held(tokens))
    return [tuple(outs[2 * k : 2 * k + 2]) for k in range(experts)]


def place_kernel(experts, capacity, steps, has_base, last, plane_ref, routes_ref, *refs):
    refs = list(refs)
    out = refs.pop()
    scale = turned(refs.pop(0)[...]) if last else None
    base = refs.pop(0) if has_base else None
    row = routes_ref[...]
    rows, width = out.shape
    slot = turned(slots_by_row(row, plane_ref[0], experts, capacity))
    first = lax.broadcasted_iota(jnp.int32, (rows, capacity), 1)
    pick = jnp.concatenate([(slot == first + k * capacity).astype(jnp.float32) for k in steps], axis=1)
    pick = pick.astype(jnp.bfloat16)
    half = width // 2
    tile = tile_of(half, 512)
    for c in range(0, width, tile):
        part, whole = pl.ds(c % half, tile), pl.ds(c, tile)
        data = [refs[2 * n + c // half][:, part] for n in range(len(steps))]
        value = jnp.dot(
            pick, jnp.concatenate(data, axis=0), preferred_element_type=jnp.float32
        )
        if has_base:
            value = value + base[:, whole]
        if last:
            value = scale * value
        out[:, whole] = value.astype(out.dtype)


def place(plane, routes, items, experts, base=None, scale=None):
    rows = routes.shape[1]
    capacity, half = items[0][1][0].shape
    width = 2 * half
    last = scale is not None
    operands = [plane, routes]
    if last:
        operands.append(scale)
    if base is not None:
        operands.append(base)
    for _, halves in items:
        operands += halves
    steps = [k for k, _ in items]
    return pl.pallas_call(
        functools.partial(place_kernel, experts, capacity, steps, base is not None, last),
        out_shape=jax.ShapeDtypeStruct((rows, width), jnp.bfloat16 if last else jnp.float32),
        in_specs=[SMEM] + [VMEM] * (len(operands) - 1),
        out_specs=VMEM,
        cost_estimate=pl.CostEstimate(
            flops=2 * rows * len(items) * capacity * width,
            bytes_accessed=2 * (rows + len(items) * capacity) * width,
            transcendentals=0,
        ),
        compiler_params=pltpu.CompilerParams(vmem_limit_bytes=12 << 20),
        name="place",
    )(*operands)


def stage_kernel(*refs):
    count = (len(refs) - 1) // 2
    sems = refs[-1]
    copies = [
        pltpu.make_async_copy(refs[i], refs[count + i], sems.at[i]) for i in range(count)
    ]
    for copy in copies:
        copy.start()
    for copy in copies:
        copy.wait()


def stage(arrays):
    return pl.pallas_call(
        stage_kernel,
        out_shape=[pltpu.VMEM(a.shape, a.dtype) for a in arrays],
        in_specs=[HBM] * len(arrays),
        out_specs=[VMEM] * len(arrays),
        scratch_shapes=[pltpu.SemaphoreType.DMA((len(arrays),))],
        cost_estimate=pl.CostEstimate(
            flops=0, bytes_accessed=4 * sum(a.size for a in arrays), transcendentals=0
        ),
        compiler_params=pltpu.CompilerParams(vmem_limit_bytes=4 << 20),
        name="stage",
    )(*[held(a) for a in arrays])


def expert_kernel(blocks, hid_tile, *refs):
    ins, refs = refs[: 2 * blocks], refs[2 * blocks :]
    weights, refs = refs[:6], refs[6:]
    outs, refs = refs[: 2 * blocks], refs[2 * blocks :]
    rows, hidden = refs
    capacity, half = ins[0].shape
    hid = hidden.shape[1] // 2
    for i in range(blocks):
        for c in range(2):
            rows[pl.ds(i * capacity, capacity), pl.ds(c * half, half)] = ins[2 * i + c][...]
    x = rows[...]
    for s in range(2):
        gate, up = weights[3 * s], weights[3 * s + 1]
        for h in range(0, hid, hid_tile):
            part = pl.ds(h, hid_tile)
            gate_val = jnp.dot(x, gate[:, part], preferred_element_type=jnp.float32)
            up_val = jnp.dot(x, up[:, part], preferred_element_type=jnp.float32)
            value = gate_val / (1.0 + jnp.exp(-gate_val)) * up_val
            hidden[:, pl.ds(s * hid + h, hid_tile)] = value.astype(jnp.bfloat16)
    tile = tile_of(half, 512)
    for c in range(0, 2 * half, tile):
        part, whole = pl.ds(c % half, tile), pl.ds(c, tile)
        value = jnp.dot(hidden[:, :hid], weights[2][:, whole], preferred_element_type=jnp.float32)
        value += jnp.dot(hidden[:, hid:], weights[5][:, whole], preferred_element_type=jnp.float32)
        value = value.astype(jnp.bfloat16)
        for i in range(blocks):
            outs[2 * i + c // half][:, part] = value[i * capacity : (i + 1) * capacity]


def run_expert(blocks, weights):
    capacity, half = blocks[0][0].shape
    count, total, width = len(blocks), len(blocks) * capacity, 2 * half
    hid = weights[0].shape[1]
    outs = pl.pallas_call(
        functools.partial(expert_kernel, count, tile_of(hid, 256)),
        out_shape=[jax.ShapeDtypeStruct((capacity, half), jnp.bfloat16)] * (2 * count),
        in_specs=[VMEM] * (2 * count + 6),
        out_specs=[VMEM] * (2 * count),
        scratch_shapes=[
            pltpu.VMEM((total, width), jnp.bfloat16),
            pltpu.VMEM((total, 2 * hid), jnp.bfloat16),
        ],
        compiler_params=pltpu.CompilerParams(vmem_limit_bytes=16 << 20),
        cost_estimate=pl.CostEstimate(
            flops=2 * total * width * hid * 6,
            bytes_accessed=12 * width * hid + 4 * total * width,
            transcendentals=total * hid * 2,
        ),
        name="expert",
    )(*[h for block in blocks for h in block], *weights)
    return [tuple(outs[2 * i : 2 * i + 2]) for i in range(count)]


def per_device(tokens, routes, gate_weights, w_gate, w_up, w_down):
    rows = tokens.shape[0]
    experts = lax.axis_size("plane")
    capacity = 2 * rows // experts
    paired = experts & (experts - 1) == 0
    plane = jnp.reshape(lax.axis_index("plane"), (1,)).astype(jnp.int32)
    routes, scale = routes.reshape(1, rows), gate_weights.reshape(1, rows)

    def there(k):
        return [(i, i ^ k if paired else (i + k) % experts) for i in range(experts)]

    def back(k):
        return [(b, a) for a, b in there(k)]

    def both(halves, axis, pairs):
        return tuple(lax.ppermute(x, axis, pairs) for x in halves)

    packed = pack(plane, routes, tokens, experts, capacity)
    own = both(packed[0], "row", SWAP)
    sent = {k: both(packed[k], "plane", there(k)) for k in range(1, experts)}
    weights = [w_gate[0], w_up[0], w_down[0]]
    other = [lax.ppermute(w, "core", SWAP) for w in weights]
    weights = [*stage(weights), *other]

    own_a, own_b = run_expert([packed[0], own], weights)
    items = [(0, own_a), (0, both(own_b, "row", SWAP))]
    for k in range(1, experts):
        met = both(sent[k], "row", SWAP)
        a, b = run_expert([sent[k], met], weights)
        b = both(b, "row", SWAP)
        total = [
            (u.astype(jnp.float32) + v.astype(jnp.float32)).astype(jnp.bfloat16)
            for u, v in zip(a, b)
        ]
        items.append((k, both(total, "plane", back(k))))
    early = [items[0]] + items[3:-1]
    late = [items[1], items[2], items[-1]]
    base = place(plane, routes, early, experts)
    return place(plane, routes, late, experts, base, scale)


def solution(mesh):
    groups, devices = mesh.shape["group"], mesh.shape["expert"]
    experts = devices // SPAN
    fine = Mesh(
        mesh.devices.reshape(groups, experts, SPAN // 2, 2), ("group", "plane", "row", "core")
    )
    every = ("group", "plane", "row", "core")
    expert = ("plane", "row", "core")
    placed = (P(every, None),) * 3 + (P(expert, None, None),) * 3

    return jax.shard_map(
        per_device, mesh=fine, in_specs=placed, out_specs=P(every, None), check_vma=False
    )
```

```python
import functools

import jax
import jax.numpy as jnp
from jax import lax
from jax.experimental import pallas as pl
from jax.experimental.pallas import tpu as pltpu
from jax.sharding import Mesh
from jax.sharding import PartitionSpec as P


SPAN = 4
SWAP = [(0, 1), (1, 0)]
SENDS = {0: 1}
RETURNS = {}
VMEM = pl.BlockSpec(memory_space=pltpu.VMEM)
SMEM = pl.BlockSpec(memory_space=pltpu.SMEM)
HBM = pl.BlockSpec(memory_space=pltpu.HBM)


def held(x):
    return pltpu.with_memory_space_constraint(x, pltpu.HBM)


def grouped(refs, counts):
    refs, groups = list(refs), []
    for n in counts:
        groups.append(refs[:n])
        refs = refs[n:]
    return groups


def window(pieces, column, tile):
    span = pieces[0].shape[1]
    return pieces[column // span], pl.ds(column % span, tile)


def tile_of(size, most):
    return max(t for t in range(128, most + 1, 128) if size % t == 0)


def steps_to(route, plane, experts):
    if experts & (experts - 1) == 0:
        return route ^ plane
    return lax.rem(route - plane + experts, experts)


def grids(rows):
    return [lax.broadcasted_iota(jnp.int32, (rows, rows), d) for d in range(2)]


def turned(row):
    rows = row.shape[1]
    sub, lane = grids(rows)
    wide = jnp.broadcast_to(row, (rows, rows))
    return jnp.sum(jnp.where(sub == lane, wide, jnp.zeros_like(wide)), axis=1, keepdims=True)


def slots_by_row(row, plane, experts, capacity):
    sub, lane = grids(row.shape[1])
    before = ((turned(row) == row) & (sub < lane)).astype(jnp.int32)
    position = jnp.sum(before, axis=0, keepdims=True)
    return steps_to(row, plane, experts) * capacity + position


def pack_kernel(counts, capacity, plane_ref, routes_ref, tokens_ref, *refs):
    outs, (routes, tokens, sems) = refs[:-3], refs[-3:]
    rows, width = tokens.shape
    half = width // 2
    first = pltpu.make_async_copy(routes_ref, routes, sems.at[2])
    first.start()
    copies = []
    for c in range(2):
        part = pl.ds(c * half, half)
        copies.append(
            pltpu.make_async_copy(tokens_ref.at[:, part], tokens.at[:, part], sems.at[c])
        )
        copies[c].start()
    first.wait()
    experts = len(counts)
    outs = grouped(outs, counts)
    slot = slots_by_row(routes[...], plane_ref[0], experts, capacity)
    every = lax.broadcasted_iota(jnp.int32, (experts * capacity, rows), 0)
    pick = (slot == every).astype(jnp.bfloat16)
    tile = tile_of(half, 512)
    for c in range(0, width, tile):
        if c % half == 0:
            copies[c // half].wait()
        value = jnp.dot(pick, tokens[:, pl.ds(c, tile)], preferred_element_type=jnp.float32)
        value = value.astype(jnp.bfloat16)
        for k in range(experts):
            out, part = window(outs[k], c, tile)
            out[:, part] = value[k * capacity : (k + 1) * capacity]


def pieces_of(counts, rows, width):
    return [jax.ShapeDtypeStruct((rows, width // n), jnp.bfloat16) for n in counts for _ in range(n)]


def pack(plane, routes, tokens, counts, capacity):
    rows, width = tokens.shape
    experts = len(counts)
    outs = pl.pallas_call(
        functools.partial(pack_kernel, counts, capacity),
        out_shape=pieces_of(counts, capacity, width),
        in_specs=[SMEM, HBM, HBM],
        out_specs=[VMEM] * sum(counts),
        scratch_shapes=[
            pltpu.VMEM(routes.shape, routes.dtype),
            pltpu.VMEM(tokens.shape, tokens.dtype),
            pltpu.SemaphoreType.DMA((3,)),
        ],
        cost_estimate=pl.CostEstimate(
            flops=2 * rows * experts * capacity * width,
            bytes_accessed=2 * (rows + experts * capacity) * width,
            transcendentals=0,
        ),
        compiler_params=pltpu.CompilerParams(vmem_limit_bytes=12 << 20),
        name="pack",
    )(plane, held(routes), held(tokens))
    return grouped(outs, counts)


def choose(routes_ref, plane_ref, steps, experts, capacity):
    row = routes_ref[...]
    slot = turned(slots_by_row(row, plane_ref[0], experts, capacity))
    first = lax.broadcasted_iota(jnp.int32, (row.shape[1], capacity), 1)
    picks = [(slot == first + k * capacity).astype(jnp.float32) for k in steps]
    return jnp.concatenate(picks, axis=1).astype(jnp.bfloat16)


def gathered(pick, blocks, column, tile):
    parts = [window(block, column, tile) for block in blocks]
    data = jnp.concatenate([piece[:, part] for piece, part in parts], axis=0)
    return jnp.dot(pick, data, preferred_element_type=jnp.float32)


def write(held, column, tile, out, sem):
    whole, part = pl.ds(column, tile), pl.ds(column % held.shape[1], tile)
    copy = pltpu.make_async_copy(held.at[:, part], out.at[:, whole], sem)
    copy.start()
    return copy


def base_kernel(experts, capacity, early, late, plane_ref, routes_ref, scale_ref, *refs):
    steps, counts = zip(*early)
    more, _ = zip(*late)
    blocks, ends, rest = grouped(refs, (sum(counts), len(late), 6))
    out, base, kept, factor, held, sems = rest
    blocks = grouped(blocks, counts)
    pick = choose(routes_ref, plane_ref, steps, experts, capacity)
    extra = choose(routes_ref, plane_ref, more, experts, capacity)
    scale = turned(scale_ref[...])
    kept[...] = extra
    factor[...] = jnp.broadcast_to(scale, factor.shape)
    half = held.shape[1]
    tile = tile_of(half, 512)
    copies = []
    for n, c in enumerate(range(0, half, tile)):
        value = gathered(pick, blocks, c, tile) + gathered(extra, [[e] for e in ends], c, tile)
        held[:, pl.ds(c, tile)] = (scale * value).astype(held.dtype)
        copies.append(write(held, c, tile, out, sems.at[n]))
    for c in range(0, half, tile):
        base[:, pl.ds(c, tile)] = gathered(pick, blocks, half + c, tile)
    for copy in copies:
        copy.wait()


def final_kernel(pick_ref, scale_ref, base, *refs):
    ends, (_, out, held, sems) = grouped(refs, (len(refs) - 4, 4))
    pick, scale = pick_ref[...], scale_ref[:, :1]
    half = held.shape[1]
    tile = tile_of(half, 512)
    copies = []
    for n, c in enumerate(range(0, half, tile)):
        value = base[:, pl.ds(c, tile)] + gathered(pick, [[e] for e in ends], c, tile)
        held[:, pl.ds(c, tile)] = (scale * value).astype(held.dtype)
        copies.append(write(held, half + c, tile, out, sems.at[n]))
    for copy in copies:
        copy.wait()


def place_left(plane, routes, scale, early, late, experts):
    rows = routes.shape[1]
    capacity, half = late[0][1][0].shape
    blocks = [piece for _, pieces in early for piece in pieces] + [p[0] for _, p in late]
    return pl.pallas_call(
        functools.partial(
            base_kernel,
            experts,
            capacity,
            [(k, len(pieces)) for k, pieces in early],
            [(k, 1) for k, _ in late],
        ),
        out_shape=[
            jax.ShapeDtypeStruct((rows, 2 * half), jnp.bfloat16),
            jax.ShapeDtypeStruct((rows, half), jnp.float32),
            jax.ShapeDtypeStruct((rows, len(late) * capacity), jnp.bfloat16),
            jax.ShapeDtypeStruct((rows, 128), jnp.float32),
        ],
        in_specs=[SMEM] + [VMEM] * (2 + len(blocks)),
        out_specs=[HBM, VMEM, VMEM, VMEM],
        scratch_shapes=[
            pltpu.VMEM((rows, half), jnp.bfloat16),
            pltpu.SemaphoreType.DMA((half // tile_of(half, 512),)),
        ],
        compiler_params=pltpu.CompilerParams(vmem_limit_bytes=12 << 20),
        name="left",
    )(plane, routes, scale, *blocks)


def place_right(out, base, pick, scale, late):
    rows, half = base.shape
    ends = [pieces[1] for _, pieces in late]
    return pl.pallas_call(
        final_kernel,
        out_shape=jax.ShapeDtypeStruct(out.shape, out.dtype),
        in_specs=[VMEM] * (3 + len(ends)) + [HBM],
        out_specs=HBM,
        scratch_shapes=[
            pltpu.VMEM((rows, half), jnp.bfloat16),
            pltpu.SemaphoreType.DMA((half // tile_of(half, 512),)),
        ],
        input_output_aliases={3 + len(ends): 0},
        compiler_params=pltpu.CompilerParams(vmem_limit_bytes=12 << 20),
        name="right",
    )(pick, scale, base, *ends, out)


def stage_kernel(*refs):
    count = (len(refs) - 1) // 2
    sems = refs[-1]
    copies = [
        pltpu.make_async_copy(refs[i], refs[count + i], sems.at[i]) for i in range(count)
    ]
    for copy in copies:
        copy.start()
    for copy in copies:
        copy.wait()


def stage(arrays):
    return pl.pallas_call(
        stage_kernel,
        out_shape=[pltpu.VMEM(a.shape, a.dtype) for a in arrays],
        in_specs=[HBM] * len(arrays),
        out_specs=[VMEM] * len(arrays),
        scratch_shapes=[pltpu.SemaphoreType.DMA((len(arrays),))],
        cost_estimate=pl.CostEstimate(
            flops=0, bytes_accessed=4 * sum(a.size for a in arrays), transcendentals=0
        ),
        compiler_params=pltpu.CompilerParams(vmem_limit_bytes=4 << 20),
        name="stage",
    )(*[held(a) for a in arrays])


def expert_kernel(in_counts, out_counts, hid_tile, *refs):
    ins, weights, outs, scratch = grouped(refs, (sum(in_counts), 6, sum(out_counts), 2))
    rows, hidden = scratch
    ins, outs = grouped(ins, in_counts), grouped(outs, out_counts)
    capacity, width = rows.shape[0] // len(ins), rows.shape[1]
    hid = hidden.shape[1] // 2
    for i, block in enumerate(ins):
        span = width // len(block)
        for c, piece in enumerate(block):
            rows[pl.ds(i * capacity, capacity), pl.ds(c * span, span)] = piece[...]
    x = rows[...]
    for s in range(2):
        gate, up = weights[3 * s], weights[3 * s + 1]
        for h in range(0, hid, hid_tile):
            part = pl.ds(h, hid_tile)
            gate_val = jnp.dot(x, gate[:, part], preferred_element_type=jnp.float32)
            up_val = jnp.dot(x, up[:, part], preferred_element_type=jnp.float32)
            value = gate_val / (1.0 + jnp.exp(-gate_val)) * up_val
            hidden[:, pl.ds(s * hid + h, hid_tile)] = value.astype(jnp.bfloat16)
    tile = tile_of(width // 2, 512)
    for c in range(0, width, tile):
        whole = pl.ds(c, tile)
        value = jnp.dot(hidden[:, :hid], weights[2][:, whole], preferred_element_type=jnp.float32)
        value += jnp.dot(hidden[:, hid:], weights[5][:, whole], preferred_element_type=jnp.float32)
        value = value.astype(jnp.bfloat16)
        for i, block in enumerate(outs):
            out, part = window(block, c, tile)
            out[:, part] = value[i * capacity : (i + 1) * capacity]


def run_expert(blocks, out_counts, weights):
    in_counts = [len(block) for block in blocks]
    capacity, width = blocks[0][0].shape[0], in_counts[0] * blocks[0][0].shape[1]
    total = len(blocks) * capacity
    hid = weights[0].shape[1]
    outs = pl.pallas_call(
        functools.partial(expert_kernel, in_counts, out_counts, tile_of(hid, 256)),
        out_shape=pieces_of(out_counts, capacity, width),
        in_specs=[VMEM] * (sum(in_counts) + 6),
        out_specs=[VMEM] * sum(out_counts),
        scratch_shapes=[
            pltpu.VMEM((total, width), jnp.bfloat16),
            pltpu.VMEM((total, 2 * hid), jnp.bfloat16),
        ],
        compiler_params=pltpu.CompilerParams(vmem_limit_bytes=16 << 20),
        cost_estimate=pl.CostEstimate(
            flops=2 * total * width * hid * 6,
            bytes_accessed=12 * width * hid + 4 * total * width,
            transcendentals=total * hid * 2,
        ),
        name="expert",
    )(*[piece for block in blocks for piece in block], *weights)
    return grouped(outs, out_counts)


def per_device(tokens, routes, gate_weights, w_gate, w_up, w_down):
    rows = tokens.shape[0]
    experts = lax.axis_size("plane")
    capacity = 2 * rows // experts
    paired = experts & (experts - 1) == 0
    plane = jnp.reshape(lax.axis_index("plane"), (1,)).astype(jnp.int32)
    routes, scale = routes.reshape(1, rows), gate_weights.reshape(1, rows)

    def there(k):
        return [(i, i ^ k if paired else (i + k) % experts) for i in range(experts)]

    def back(k):
        return [(b, a) for a, b in there(k)]

    def moves(pieces, axis, pairs):
        return [lax.ppermute(x, axis, pairs) for x in pieces]

    sends = [SENDS.get(k, 2) for k in range(experts)]
    packed = pack(plane, routes, tokens, sends, capacity)
    own = moves(packed[0], "row", SWAP)
    sent = {k: moves(packed[k], "plane", there(k)) for k in range(1, experts)}
    weights = [w_gate[0], w_up[0], w_down[0]]
    other = [lax.ppermute(w, "core", SWAP) for w in weights]
    weights = [*stage(weights), *other]

    own_a, own_b = run_expert([packed[0], own], [1, RETURNS.get(0, 2)], weights)
    items = [(0, own_a), (0, moves(own_b, "row", SWAP))]
    for k in range(1, experts):
        met = moves(sent[k], "row", SWAP)
        count = RETURNS.get(k, 2)
        a, b = run_expert([sent[k], met], [count, count], weights)
        b = moves(b, "row", SWAP)
        total = [
            (u.astype(jnp.float32) + v.astype(jnp.float32)).astype(jnp.bfloat16)
            for u, v in zip(a, b)
        ]
        items.append((k, moves(total, "plane", back(k))))
    early = [items[0]] + items[3:-1]
    late = [items[1], items[2], items[-1]]
    left = place_left(plane, routes, scale, early, late, experts)
    return place_right(*left, late)


def solution(mesh):
    groups, devices = mesh.shape["group"], mesh.shape["expert"]
    experts = devices // SPAN
    fine = Mesh(
        mesh.devices.reshape(groups, experts, SPAN // 2, 2), ("group", "plane", "row", "core")
    )
    every = ("group", "plane", "row", "core")
    expert = ("plane", "row", "core")
    placed = (P(every, None),) * 3 + (P(expert, None, None),) * 3

    return jax.shard_map(
        per_device, mesh=fine, in_specs=placed, out_specs=P(every, None), check_vma=False
    )
```

```python
import functools

import jax
import jax.numpy as jnp
from jax import lax
from jax.experimental import pallas as pl
from jax.experimental.pallas import tpu as pltpu
from jax.sharding import Mesh
from jax.sharding import PartitionSpec as P


SPAN = 4
SWAP = [(0, 1), (1, 0)]
SENDS = {0: 1}
RETURNS = {}
VMEM = pl.BlockSpec(memory_space=pltpu.VMEM)
SMEM = pl.BlockSpec(memory_space=pltpu.SMEM)
HBM = pl.BlockSpec(memory_space=pltpu.HBM)


def held(x):
    return pltpu.with_memory_space_constraint(x, pltpu.HBM)


def grouped(refs, counts):
    refs, groups = list(refs), []
    for n in counts:
        groups.append(refs[:n])
        refs = refs[n:]
    return groups


def window(pieces, column, tile):
    span = pieces[0].shape[1]
    return pieces[column // span], pl.ds(column % span, tile)


def tile_of(size, most):
    return max(t for t in range(128, most + 1, 128) if size % t == 0)


def steps_to(route, plane, experts):
    if experts & (experts - 1) == 0:
        return route ^ plane
    return lax.rem(route - plane + experts, experts)


def grids(rows):
    return [lax.broadcasted_iota(jnp.int32, (rows, rows), d) for d in range(2)]


def turned(row):
    rows = row.shape[1]
    sub, lane = grids(rows)
    wide = jnp.broadcast_to(row, (rows, rows))
    return jnp.sum(jnp.where(sub == lane, wide, jnp.zeros_like(wide)), axis=1, keepdims=True)


def slots_by_row(row, plane, experts, capacity):
    sub, lane = grids(row.shape[1])
    before = ((turned(row) == row) & (sub < lane)).astype(jnp.int32)
    position = jnp.sum(before, axis=0, keepdims=True)
    return steps_to(row, plane, experts) * capacity + position


def pack_kernel(counts, capacity, plane_ref, routes_ref, tokens_ref, *refs):
    outs, (routes, tokens, sems) = refs[:-3], refs[-3:]
    rows, width = tokens.shape
    half = width // 2
    first = pltpu.make_async_copy(routes_ref, routes, sems.at[4])
    first.start()
    tile = tile_of(half, 512)
    copies = {}
    for n, c in enumerate((0, tile, half, half + 3 * tile)):
        end = (tile, half, half + 3 * tile, width)[n]
        part = pl.ds(c, end - c)
        copies[c] = pltpu.make_async_copy(tokens_ref.at[:, part], tokens.at[:, part], sems.at[n])
        copies[c].start()
    first.wait()
    experts = len(counts)
    outs = grouped(outs, counts)
    slot = slots_by_row(routes[...], plane_ref[0], experts, capacity)
    every = lax.broadcasted_iota(jnp.int32, (experts * capacity, rows), 0)
    pick = (slot == every).astype(jnp.bfloat16)
    tile = tile_of(half, 512)
    for c in range(0, width, tile):
        if c in copies:
            copies[c].wait()
        value = jnp.dot(pick, tokens[:, pl.ds(c, tile)], preferred_element_type=jnp.float32)
        value = value.astype(jnp.bfloat16)
        for k in range(experts):
            out, part = window(outs[k], c, tile)
            out[:, part] = value[k * capacity : (k + 1) * capacity]


def pieces_of(counts, rows, width):
    return [jax.ShapeDtypeStruct((rows, width // n), jnp.bfloat16) for n in counts for _ in range(n)]


def pack(plane, routes, tokens, counts, capacity):
    rows, width = tokens.shape
    experts = len(counts)
    outs = pl.pallas_call(
        functools.partial(pack_kernel, counts, capacity),
        out_shape=pieces_of(counts, capacity, width),
        in_specs=[SMEM, HBM, HBM],
        out_specs=[VMEM] * sum(counts),
        scratch_shapes=[
            pltpu.VMEM(routes.shape, routes.dtype),
            pltpu.VMEM(tokens.shape, tokens.dtype),
            pltpu.SemaphoreType.DMA((5,)),
        ],
        cost_estimate=pl.CostEstimate(
            flops=2 * rows * experts * capacity * width,
            bytes_accessed=2 * (rows + experts * capacity) * width,
            transcendentals=0,
        ),
        compiler_params=pltpu.CompilerParams(vmem_limit_bytes=12 << 20),
        name="pack",
    )(plane, held(routes), held(tokens))
    return grouped(outs, counts)


def choose(routes_ref, plane_ref, steps, experts, capacity):
    row = routes_ref[...]
    slot = turned(slots_by_row(row, plane_ref[0], experts, capacity))
    first = lax.broadcasted_iota(jnp.int32, (row.shape[1], capacity), 1)
    picks = [(slot == first + k * capacity).astype(jnp.float32) for k in steps]
    return jnp.concatenate(picks, axis=1).astype(jnp.bfloat16)


def gathered(pick, blocks, column, tile):
    parts = [window(block, column, tile) for block in blocks]
    data = jnp.concatenate([piece[:, part] for piece, part in parts], axis=0)
    return jnp.dot(pick, data, preferred_element_type=jnp.float32)


def write(held, column, tile, out, sem):
    whole, part = pl.ds(column, tile), pl.ds(column % held.shape[1], tile)
    copy = pltpu.make_async_copy(held.at[:, part], out.at[:, whole], sem)
    copy.start()
    return copy


def base_kernel(experts, capacity, early, late, plane_ref, routes_ref, scale_ref, *refs):
    steps, counts = zip(*early)
    more, _ = zip(*late)
    blocks, ends, rest = grouped(refs, (sum(counts), len(late), 6))
    out, base, kept, factor, held, sems = rest
    blocks = grouped(blocks, counts)
    pick = choose(routes_ref, plane_ref, steps, experts, capacity)
    extra = choose(routes_ref, plane_ref, more, experts, capacity)
    scale = turned(scale_ref[...])
    kept[...] = extra
    factor[...] = jnp.broadcast_to(scale, factor.shape)
    half = held.shape[1]
    tile = tile_of(half, 512)
    copies = []
    for n, c in enumerate(range(0, half, tile)):
        value = gathered(pick, blocks, c, tile) + gathered(extra, [[e] for e in ends], c, tile)
        held[:, pl.ds(c, tile)] = (scale * value).astype(held.dtype)
        copies.append(write(held, c, tile, out, sems.at[n]))
    for c in range(0, half, tile):
        base[:, pl.ds(c, tile)] = gathered(pick, blocks, half + c, tile)
    for copy in copies:
        copy.wait()


def final_kernel(pick_ref, scale_ref, base, *refs):
    ends, (_, out, held, sems) = grouped(refs, (len(refs) - 4, 4))
    pick, scale = pick_ref[...], scale_ref[:, :1]
    half = held.shape[1]
    tile = tile_of(half, 512)
    copies = []
    for n, c in enumerate(range(0, half, tile)):
        value = base[:, pl.ds(c, tile)] + gathered(pick, [[e] for e in ends], c, tile)
        held[:, pl.ds(c, tile)] = (scale * value).astype(held.dtype)
        copies.append(write(held, half + c, tile, out, sems.at[n]))
    for copy in copies:
        copy.wait()


def place_left(plane, routes, scale, early, late, experts):
    rows = routes.shape[1]
    capacity, half = late[0][1][0].shape
    blocks = [piece for _, pieces in early for piece in pieces] + [p[0] for _, p in late]
    return pl.pallas_call(
        functools.partial(
            base_kernel,
            experts,
            capacity,
            [(k, len(pieces)) for k, pieces in early],
            [(k, 1) for k, _ in late],
        ),
        out_shape=[
            jax.ShapeDtypeStruct((rows, 2 * half), jnp.bfloat16),
            jax.ShapeDtypeStruct((rows, half), jnp.float32),
            jax.ShapeDtypeStruct((rows, len(late) * capacity), jnp.bfloat16),
            jax.ShapeDtypeStruct((rows, 128), jnp.float32),
        ],
        in_specs=[SMEM] + [VMEM] * (2 + len(blocks)),
        out_specs=[HBM, VMEM, VMEM, VMEM],
        scratch_shapes=[
            pltpu.VMEM((rows, half), jnp.bfloat16),
            pltpu.SemaphoreType.DMA((half // tile_of(half, 512),)),
        ],
        compiler_params=pltpu.CompilerParams(vmem_limit_bytes=12 << 20),
        name="left",
    )(plane, routes, scale, *blocks)


def place_right(out, base, pick, scale, late):
    rows, half = base.shape
    ends = [pieces[1] for _, pieces in late]
    return pl.pallas_call(
        final_kernel,
        out_shape=jax.ShapeDtypeStruct(out.shape, out.dtype),
        in_specs=[VMEM] * (3 + len(ends)) + [HBM],
        out_specs=HBM,
        scratch_shapes=[
            pltpu.VMEM((rows, half), jnp.bfloat16),
            pltpu.SemaphoreType.DMA((half // tile_of(half, 512),)),
        ],
        input_output_aliases={3 + len(ends): 0},
        compiler_params=pltpu.CompilerParams(vmem_limit_bytes=12 << 20),
        name="right",
    )(pick, scale, base, *ends, out)


def stage_kernel(*refs):
    count = (len(refs) - 1) // 2
    sems = refs[-1]
    copies = [
        pltpu.make_async_copy(refs[i], refs[count + i], sems.at[i]) for i in range(count)
    ]
    for copy in copies:
        copy.start()
    for copy in copies:
        copy.wait()


def stage(arrays):
    return pl.pallas_call(
        stage_kernel,
        out_shape=[pltpu.VMEM(a.shape, a.dtype) for a in arrays],
        in_specs=[HBM] * len(arrays),
        out_specs=[VMEM] * len(arrays),
        scratch_shapes=[pltpu.SemaphoreType.DMA((len(arrays),))],
        cost_estimate=pl.CostEstimate(
            flops=0, bytes_accessed=4 * sum(a.size for a in arrays), transcendentals=0
        ),
        compiler_params=pltpu.CompilerParams(vmem_limit_bytes=4 << 20),
        name="stage",
    )(*[held(a) for a in arrays])


def expert_kernel(in_counts, out_counts, hid_tile, *refs):
    ins, weights, outs, scratch = grouped(refs, (sum(in_counts), 6, sum(out_counts), 2))
    rows, hidden = scratch
    ins, outs = grouped(ins, in_counts), grouped(outs, out_counts)
    capacity, width = rows.shape[0] // len(ins), rows.shape[1]
    hid = hidden.shape[1] // 2
    for i, block in enumerate(ins):
        span = width // len(block)
        for c, piece in enumerate(block):
            rows[pl.ds(i * capacity, capacity), pl.ds(c * span, span)] = piece[...]
    x = rows[...]
    for s in range(2):
        gate, up = weights[3 * s], weights[3 * s + 1]
        for h in range(0, hid, hid_tile):
            part = pl.ds(h, hid_tile)
            gate_val = jnp.dot(x, gate[:, part], preferred_element_type=jnp.float32)
            up_val = jnp.dot(x, up[:, part], preferred_element_type=jnp.float32)
            value = gate_val / (1.0 + jnp.exp(-gate_val)) * up_val
            hidden[:, pl.ds(s * hid + h, hid_tile)] = value.astype(jnp.bfloat16)
    tile = tile_of(width // 2, 512)
    for c in range(0, width, tile):
        whole = pl.ds(c, tile)
        value = jnp.dot(hidden[:, :hid], weights[2][:, whole], preferred_element_type=jnp.float32)
        value += jnp.dot(hidden[:, hid:], weights[5][:, whole], preferred_element_type=jnp.float32)
        value = value.astype(jnp.bfloat16)
        for i, block in enumerate(outs):
            out, part = window(block, c, tile)
            out[:, part] = value[i * capacity : (i + 1) * capacity]


def run_expert(blocks, out_counts, weights):
    in_counts = [len(block) for block in blocks]
    capacity, width = blocks[0][0].shape[0], in_counts[0] * blocks[0][0].shape[1]
    total = len(blocks) * capacity
    hid = weights[0].shape[1]
    outs = pl.pallas_call(
        functools.partial(expert_kernel, in_counts, out_counts, tile_of(hid, 256)),
        out_shape=pieces_of(out_counts, capacity, width),
        in_specs=[VMEM] * (sum(in_counts) + 6),
        out_specs=[VMEM] * sum(out_counts),
        scratch_shapes=[
            pltpu.VMEM((total, width), jnp.bfloat16),
            pltpu.VMEM((total, 2 * hid), jnp.bfloat16),
        ],
        compiler_params=pltpu.CompilerParams(vmem_limit_bytes=16 << 20),
        cost_estimate=pl.CostEstimate(
            flops=2 * total * width * hid * 6,
            bytes_accessed=12 * width * hid + 4 * total * width,
            transcendentals=total * hid * 2,
        ),
        name="expert",
    )(*[piece for block in blocks for piece in block], *weights)
    return grouped(outs, out_counts)


def per_device(tokens, routes, gate_weights, w_gate, w_up, w_down):
    rows = tokens.shape[0]
    experts = lax.axis_size("plane")
    capacity = 2 * rows // experts
    paired = experts & (experts - 1) == 0
    plane = jnp.reshape(lax.axis_index("plane"), (1,)).astype(jnp.int32)
    routes, scale = routes.reshape(1, rows), gate_weights.reshape(1, rows)

    def there(k):
        return [(i, i ^ k if paired else (i + k) % experts) for i in range(experts)]

    def back(k):
        return [(b, a) for a, b in there(k)]

    def moves(pieces, axis, pairs):
        return [lax.ppermute(x, axis, pairs) for x in pieces]

    sends = [SENDS.get(k, 2) for k in range(experts)]
    packed = pack(plane, routes, tokens, sends, capacity)
    own = moves(packed[0], "row", SWAP)
    sent = {k: moves(packed[k], "plane", there(k)) for k in range(1, experts)}
    weights = [w_gate[0], w_up[0], w_down[0]]
    other = [lax.ppermute(w, "core", SWAP) for w in weights]
    weights = [*stage(weights), *other]

    own_a, own_b = run_expert([packed[0], own], [1, RETURNS.get(0, 2)], weights)
    items = [(0, own_a), (0, moves(own_b, "row", SWAP))]
    for k in range(1, experts):
        met = moves(sent[k], "row", SWAP)
        count = RETURNS.get(k, 2)
        a, b = run_expert([sent[k], met], [count, count], weights)
        b = moves(b, "row", SWAP)
        total = [
            (u.astype(jnp.float32) + v.astype(jnp.float32)).astype(jnp.bfloat16)
            for u, v in zip(a, b)
        ]
        items.append((k, moves(total, "plane", back(k))))
    early = [items[0]] + items[3:-1]
    late = [items[1], items[2], items[-1]]
    left = place_left(plane, routes, scale, early, late, experts)
    return place_right(*left, late)


def solution(mesh):
    groups, devices = mesh.shape["group"], mesh.shape["expert"]
    experts = devices // SPAN
    fine = Mesh(
        mesh.devices.reshape(groups, experts, SPAN // 2, 2), ("group", "plane", "row", "core")
    )
    every = ("group", "plane", "row", "core")
    expert = ("plane", "row", "core")
    placed = (P(every, None),) * 3 + (P(expert, None, None),) * 3

    return jax.shard_map(
        per_device, mesh=fine, in_specs=placed, out_specs=P(every, None), check_vma=False
    )
```
